32 devices in a mesh: dp: 8 (over z, y), vocab: 4 (over x, core).
Axes of the slice: x: 2, y: 2, z: 4, core: 2. Of those that a mesh axis runs over, the one named last changes fastest.
Arguments:
- hidden_in: bfloat16 [64, 24, 1024], P(('dp', 'vocab')), may hold values from -6 to 6
- tokens: int32 [64, 24], P(('dp', 'vocab')), may hold values from 0 to 131071
- lengths: int32 [64], P(('dp', 'vocab')), may hold values from 2 to 24, as said below
- cutoff: int32 [1], replicated, may hold values from 1 to 64
- norm_gain: float32 [1024], replicated, may hold values from 0.5 to 1.5
- gate_weight: bfloat16 [1024, 4096], P(None, 'vocab'), may hold values from -0.1875 to 0.1875
- up_weight: bfloat16 [1024, 4096], P(None, 'vocab'), may hold values from -0.1875 to 0.1875
- down_weight: bfloat16 [4096, 1024], P('vocab'), may hold values from -0.09375 to 0.09375
- final_gain: float32 [1024], replicated, may hold values from 0.5 to 1.5
- head_table: bfloat16 [131072, 1024], P(('dp', 'vocab')), may hold values from -12 to 12
Outputs:
- log_ppl: float32 [64], P(('dp', 'vocab'))
- margin: float32 [64], P(('dp', 'vocab'))
The draws below stay inside these ranges and needn't reach their ends.
Inputs may be any that keep to these rules, and one draw needn't show every extreme that they name: Every length is 2 or more; the documents of one device have together at most 32 positions below their lengths, and some device has exactly 32.
All inputs are finite; a program needn't handle non-finite values.
Results may differ from the reference program's by a relative error of at most 0.025.
Values may be sent and summed in bfloat16 or wider, within the bound.
A program may use at most 64 MiB of HBM per device.

```python
import math
import jax
import jax.numpy as jnp
import numpy as np
from jax import lax

D = 1024
FF = 4096
V = 131072
L = 24
CAP = 32
DOCS = 64


def draw_lengths(key, part):
    pairs = DOCS // 2
    keys = jax.random.split(jax.random.fold_in(key, 23), 4)
    former = jax.random.randint(keys[0], (pairs,), 2, L + 1)
    room = jnp.minimum(L, CAP - former)
    latter = jax.random.randint(keys[1], (pairs,), 2, room + 1)
    chosen = jax.random.randint(keys[2], (), 0, pairs)
    index_pair = jnp.arange(pairs)
    former = jnp.where(index_pair == chosen, L, former)
    latter = jnp.where(index_pair == chosen, CAP - L, latter)
    swapped = jax.random.randint(keys[3], (pairs,), 0, 2)
    head_len = jnp.where(swapped == 1, latter, former)
    tail_len = jnp.where(swapped == 1, former, latter)
    return jnp.stack([head_len, tail_len], axis=1).reshape(DOCS).astype(jnp.int32)


def draw_head_table(key, part):
    keys = jax.random.split(jax.random.fold_in(key, 37), 1)
    base = jnp.clip(jax.random.normal(keys[0], (V, D), jnp.float32), -6.0, 6.0) * (3.0 / math.sqrt(D))
    base = jnp.clip(base, -12.0, 12.0)
    return base.astype(jnp.bfloat16)


def with_ends(values, rng, low, high):
    longest = values.shape.index(max(values.shape))
    spots = []
    for shift in (0, 1):
        where = [jax.random.randint(jax.random.fold_in(rng, axis), (), 0, length) for axis, length in enumerate(values.shape)]
        where[longest] = (where[longest] + shift) % values.shape[longest]
        spots.append(tuple(where))
    return values.at[spots[0]].set(low).at[spots[1]].set(high)


def levels(rng, dims, cuts, low, largest):
    loudness = 1.0
    for axis_at, shards_of in cuts:
        steps = jax.random.uniform(jax.random.fold_in(jax.random.fold_in(rng, 6), axis_at), (shards_of,), jnp.float32, low / len(cuts), largest / len(cuts))
        loudness = loudness * jnp.repeat(jnp.exp(steps), dims[axis_at] // shards_of).reshape((-1,) + (1,) * (len(dims) - 1 - axis_at))
    return loudness


def ranked_wide(own_key, extent, count, lean):
    loads = [min(1 << octave, count + 1 - (1 << octave)) * (1 << 20) // math.isqrt((1 << octave) ** lean) + 1 for octave in range((count + 1).bit_length()) if 1 << octave <= count]
    deviation = 1 + sum(loads) // (1 << 30)
    table = np.cumsum(np.array([max(1, weight // deviation) for weight in loads]))
    ticket = jax.random.randint(jax.random.fold_in(own_key, 1), extent, 0, int(table[len(loads) - 1]))
    start = jnp.left_shift(1, jnp.searchsorted(jnp.asarray(table, jnp.int32), ticket, side="right").astype(jnp.int32))
    rank = start - 1 + jax.random.randint(jax.random.fold_in(own_key, 4), extent, 0, 1 << 30) % jnp.minimum(start, count + 1 - start)
    return jax.random.permutation(jax.random.fold_in(own_key, 2), count)[rank].astype(jnp.int32)


def centred(own_key, extent, width, reach, shards=(), kind=jnp.bfloat16):
    entries = width * jax.random.normal(own_key, extent, jnp.float32)
    if shards:
        entries = entries * levels(own_key, extent, shards, -0.22, 0.18)
    return jnp.clip(entries, -reach, reach).astype(kind)


def setup_inputs(seed: int = 0) -> dict:
    key_of = jax.random.split(jax.random.key(seed), 11)
    return {
        "hidden_in": centred(key_of[0], (DOCS, L, D), 1.0, 6.0, ((0, 32),)),
        "tokens": with_ends(ranked_wide(key_of[1], (DOCS, L), V, 2), jax.random.fold_in(key_of[1], 3), 0, V - 1).astype(jnp.int32),
        "lengths": draw_lengths(jax.random.fold_in(key_of[10], 71), 0),
        "cutoff": jax.random.randint(key_of[3], (1,), 1, DOCS + 1).astype(jnp.int32),
        "norm_gain": jnp.clip(jax.random.uniform(key_of[4], (D,), jnp.float32, 0.5, 1.5), 0.5, 1.5),
        "gate_weight": centred(key_of[5], (D, FF), D ** -0.5, 0.1875, ((1, 4),)),
        "up_weight": centred(key_of[6], (D, FF), D ** -0.5, 0.1875, ((1, 4),)),
        "down_weight": centred(key_of[7], (FF, D), FF ** -0.5, 0.09375, ((0, 4),)),
        "final_gain": jnp.clip(jax.random.uniform(key_of[8], (D,), jnp.float32, 0.5, 1.5), 0.5, 1.5),
        "head_table": draw_head_table(jax.random.fold_in(key_of[10], 71), 0),
    }


def rms_norm(values, gain):
    squares = lax.optimization_barrier(jnp.mean(values * values, axis=-1, keepdims=True))
    return values * lax.rsqrt(squares + 1e-06) * gain

def reference(hidden_in, tokens, lengths, cutoff, norm_gain, gate_weight, up_weight, down_weight, final_gain, head_table):
    residual = hidden_in.reshape(-1, D).astype(jnp.float32)
    normed = rms_norm(residual, norm_gain).astype(jnp.bfloat16)
    gate_part = jnp.dot(normed, gate_weight, preferred_element_type=jnp.float32)
    up_part = jnp.dot(normed, up_weight, preferred_element_type=jnp.float32)
    active = (jax.nn.silu(gate_part) * up_part).astype(jnp.bfloat16)
    stream = (residual + jnp.dot(active, down_weight, preferred_element_type=jnp.float32)).astype(jnp.bfloat16)
    final_rows = rms_norm(stream.astype(jnp.float32), final_gain).astype(jnp.bfloat16)
    targets = jnp.concatenate([tokens[:, 1:], tokens[:, :1]], axis=1).reshape(-1).astype(jnp.int32)
    row_total = final_rows.shape[0]
    block_size = math.gcd(row_total, 256)

    def score_block(block_pair):
        block_part, block_targets = block_pair
        logits = lax.dot_general(block_part, head_table, (((1,), (1,)), ((), ())), preferred_element_type=jnp.float32)
        highest = lax.optimization_barrier(jnp.max(logits, axis=1))
        exp_sum = lax.optimization_barrier(jnp.sum(jnp.exp(logits - highest[:, None]), axis=1))
        picked = jnp.take_along_axis(logits, block_targets[:, None], axis=1)[:, 0]
        return highest + jnp.log(exp_sum) - picked
    nll = lax.map(score_block, (final_rows.reshape(row_total // block_size, block_size, D), targets.reshape(row_total // block_size, block_size)))
    nll = nll.reshape(DOCS, L)
    position = jnp.arange(L, dtype=jnp.int32)
    live_mask = position[None, :] < lengths[:, None] - 1
    log_ppl = lax.optimization_barrier(jnp.sum(jnp.where(live_mask, nll, 0.0), axis=1)) / (lengths - 1).astype(nll.dtype)
    ordered = jnp.sort(log_ppl)
    threshold = lax.dynamic_index_in_dim(ordered, (cutoff[0] - 1).astype(jnp.int32), 0, keepdims=False)
    return (log_ppl, log_ppl - threshold)
```

```python
import functools

import jax
import jax.numpy as jnp
from jax import lax
from jax.experimental import pallas as pl
from jax.experimental.pallas import tpu as pltpu
from jax.sharding import PartitionSpec as P

MESH = pl.DeviceIdType.MESH
CAP = 32
LANES = 128


def rms_norm(values, gain):
    squares = jnp.mean(values * values, axis=-1, keepdims=True)
    return values * lax.rsqrt(squares + 1e-06) * gain


def kernel(
    dp_size, vocab_size, docs, length,
    hidden_ref, tokens_ref, lengths_ref, cutoff_ref, norm_gain_ref, final_gain_ref,
    gate_hbm, up_hbm, down_hbm, table_hbm,
    ppl_ref, margin_ref,
    gate, up, down, table, group_rows, acc, part_out, part_in, rows, targets_out, targets_in,
    stats_out, stats_in, ppl_out, ppl_in,
    local_sem, group_send, group_recv, part_send, part_recv, row_send, row_recv,
    target_send, target_recv, stat_send, stat_recv, ppl_send, ppl_recv,
):
    dp = lax.axis_index("dp")
    vocab = lax.axis_index("vocab")
    count = dp_size * vocab_size
    z_size = dp_size // 2
    z, y = dp // 2, dp % 2
    x, c = vocab // 2, vocab % 2
    width = hidden_ref.shape[1]
    vocab_rows = table.shape[0]
    per_lane = LANES // CAP

    def block_of(y, x, c, z):
        return ((y * 2 + x) * 2 + c) * z_size + z

    def device_of(block):
        rest = block // z_size
        return (
            (block % z_size) * 2 + rest // 4,
            ((rest // 2) % 2) * 2 + rest % 2,
        )

    me = block_of(y, x, c, z)
    lane_start = (me % per_lane) * CAP

    local = [
        pltpu.make_async_copy(source, target, local_sem.at[i])
        for i, (source, target) in enumerate(
            ((gate_hbm, gate), (up_hbm, up), (down_hbm, down), (table_hbm, table))
        )
    ]
    for copy in local:
        copy.start()

    barrier = pltpu.get_barrier_semaphore()

    def greet(k, carry):
        pl.semaphore_signal(
            barrier, inc=1, device_id=device_of((me + k) % count), device_id_type=MESH
        )
        return carry

    lax.fori_loop(1, count, greet, 0)

    live = [lengths_ref[i] - 1 for i in range(docs)]
    base = [0]
    for i in range(docs - 1):
        base.append(base[-1] + live[i])
    slot = lax.broadcasted_iota(jnp.int32, (CAP, docs * length), 0)
    position = lax.broadcasted_iota(jnp.int32, (CAP, docs * length), 1)
    chosen = jnp.zeros((CAP, docs * length), jnp.float32)
    lane = lax.broadcasted_iota(jnp.int32, (1, LANES), 1)
    my_slot = lane - lane_start
    target = jnp.zeros((1, LANES), jnp.int32)
    for i in range(docs):
        step = position - i * length
        hit = (step >= 0) & (step < live[i]) & (slot == step + base[i])
        chosen = jnp.where(hit, 1.0, chosen)
        for t in range(length - 1):
            here = (my_slot == base[i] + t) & (t < live[i])
            target = jnp.where(here, tokens_ref[i, t + 1], target)
    packed = jnp.dot(
        chosen.astype(jnp.bfloat16), hidden_ref[...], preferred_element_type=jnp.float32
    )
    group_rows[vocab] = packed.astype(jnp.bfloat16)
    targets_out[...] = target
    targets_in[me] = target

    pl.semaphore_wait(barrier, count - 1)

    def group_copy(buffer_from, buffer_to, send, recv, k):
        other = (vocab + k) % vocab_size
        return pltpu.make_async_remote_copy(
            src_ref=buffer_from(other),
            dst_ref=buffer_to,
            send_sem=send.at[k],
            recv_sem=recv.at[k],
            device_id=(dp, other),
            device_id_type=MESH,
        )

    shares = [
        group_copy(lambda other: group_rows.at[vocab], group_rows.at[vocab], group_send, group_recv, k)
        for k in range(1, vocab_size)
    ]
    for copy in shares:
        copy.start()

    def everyone(source, landing, send, recv):
        def make(k):
            block = (me + k) % count
            return pltpu.make_async_remote_copy(
                src_ref=source(block),
                dst_ref=landing,
                send_sem=send.at[k],
                recv_sem=recv.at[k],
                device_id=device_of(block),
                device_id_type=MESH,
            )

        def start(k, carry):
            make(k).start()
            return carry

        def finish(k, carry):
            make(k).wait()
            return carry

        return start, finish

    target_start, target_finish = everyone(
        lambda block: targets_out, targets_in.at[me], target_send, target_recv
    )
    lax.fori_loop(1, count, target_start, 0)

    for copy in shares:
        copy.wait()
    for copy in local[:3]:
        copy.wait()

    all_rows = vocab_size * CAP
    normed = rms_norm(
        group_rows[...].reshape(all_rows, width).astype(jnp.float32), norm_gain_ref[...]
    ).astype(jnp.bfloat16)
    hidden_units = gate.shape[1]
    tile = min(256, hidden_units)
    for j in range(hidden_units // tile):
        units = pl.ds(j * tile, tile)
        gate_part = jnp.dot(normed, gate[:, units], preferred_element_type=jnp.float32)
        up_part = jnp.dot(normed, up[:, units], preferred_element_type=jnp.float32)
        active = (gate_part / (1.0 + jnp.exp(-gate_part)) * up_part).astype(jnp.bfloat16)
        share = jnp.dot(active, down[units, :], preferred_element_type=jnp.float32)
        if j == 0:
            acc[...] = share
        else:
            acc[...] += share
    part_out[...] = acc[...].reshape(vocab_size, CAP, width).astype(jnp.bfloat16)
    parts = [
        group_copy(lambda other: part_out.at[other], part_in.at[vocab], part_send, part_recv, k)
        for k in range(1, vocab_size)
    ]
    for copy in parts:
        copy.start()
    branch = acc[pl.ds(pl.multiple_of(vocab * CAP, CAP), CAP), :]
    for k, copy in enumerate(parts):
        copy.wait_recv()
        branch = branch + part_in[(vocab + vocab_size - 1 - k) % vocab_size].astype(jnp.float32)
    stream = (packed + branch).astype(jnp.bfloat16).astype(jnp.float32)
    rows[me] = rms_norm(stream, final_gain_ref[...]).astype(jnp.bfloat16)

    pending = []

    def send_row(block, device):
        copy = pltpu.make_async_remote_copy(
            src_ref=rows.at[block],
            dst_ref=rows.at[block],
            send_sem=row_send.at[len(pending)],
            recv_sem=row_recv.at[block],
            device_id=device,
            device_id_type=MESH,
        )
        copy.start()
        pending.append(copy)

    def wait_row(block):
        pltpu.make_async_remote_copy(
            src_ref=rows.at[block],
            dst_ref=rows.at[block],
            send_sem=row_send.at[0],
            recv_sem=row_recv.at[block],
            device_id=(dp, vocab),
            device_id_type=MESH,
        ).wait_recv()

    other_core = (dp, x * 2 + 1 - c)
    y_peer = (z * 2 + 1 - y, vocab)
    x_peer = (dp, (1 - x) * 2 + c)
    half = z_size // 2

    for k in range(1, z_size):
        send_row(me, (((z + k) % z_size) * 2 + y, vocab))
    send_row(me, y_peer)
    send_row(me, x_peer)
    send_row(me, other_core)

    def relay(k):
        there = (z + k) % z_size
        if k:
            block = block_of(y, x, c, there)
            wait_row(block)
            send_row(block, y_peer)
            send_row(block, x_peer)
            send_row(block, other_core)
        block_y = block_of(1 - y, x, c, there)
        wait_row(block_y)
        if k < half:
            send_row(block_y, x_peer)
        send_row(block_y, other_core)
        block_x = block_of(y, 1 - x, c, there)
        wait_row(block_x)
        if k >= half:
            send_row(block_x, y_peer)
        send_row(block_x, other_core)

    def relay_diagonal():
        for k in range(z_size):
            block = block_of(1 - y, 1 - x, c, (z + k) % z_size)
            wait_row(block)
            send_row(block, other_core)

    def wait_core(y, x):
        for k in range(z_size):
            wait_row(block_of(y, x, 1 - c, k))

    offset = (dp * vocab_size + vocab) * vocab_rows
    chunk = min(1024, vocab_rows)
    set_blocks = min(8, 2 * z_size)
    set_rows = set_blocks * CAP
    lane_sets = set_rows // LANES

    def score(y, x):
        def one_set(s, carry):
            first = block_of(y, x, 0, 0) + s * set_blocks
            wanted = jnp.concatenate(
                [
                    jnp.sum(targets_in[pl.ds(first + g * per_lane, per_lane)], axis=0)
                    for g in range(lane_sets)
                ],
                axis=1,
            ) - offset
            sublane = lax.broadcasted_iota(jnp.int32, (8, set_rows), 0)
            wanted = jnp.broadcast_to(wanted, (8, set_rows)) - sublane
            index = lax.broadcasted_iota(jnp.int32, (chunk // 8, 8, set_rows), 0) * 8

            def one_chunk(j, running):
                highest, exp_sum, picked = running
                start = pl.multiple_of(j * chunk, chunk)
                part = rows[pl.ds(first, set_blocks)].reshape(set_rows, width)
                logits = lax.dot_general(
                    table[pl.ds(start, chunk), :],
                    part,
                    (((1,), (1,)), ((), ())),
                    preferred_element_type=jnp.float32,
                ).reshape(chunk // 8, 8, set_rows)
                fresh = jnp.maximum(highest, jnp.max(logits, axis=0))
                exp_sum = exp_sum * jnp.exp(highest - fresh) + jnp.sum(
                    jnp.exp(logits - fresh[None]), axis=0
                )
                picked = picked + jnp.sum(
                    jnp.where(index == (wanted - start)[None], logits, 0.0), axis=0
                )
                return fresh, exp_sum, picked

            blank = jnp.zeros((8, set_rows), jnp.float32)
            highest, exp_sum, picked = lax.fori_loop(
                0, vocab_rows // chunk, one_chunk, (blank - 3e38, blank, blank)
            )
            top = jnp.max(highest, axis=0, keepdims=True)
            total = jnp.sum(exp_sum * jnp.exp(highest - top), axis=0, keepdims=True)
            both = jnp.concatenate(
                [top + jnp.log(total), jnp.sum(picked, axis=0, keepdims=True)], axis=0
            )
            for g in range(lane_sets):
                stats_out[first // per_lane + g] = both[:, g * LANES : (g + 1) * LANES]
            return carry

        lax.fori_loop(0, 2 * z_size // set_blocks, one_set, 0)

    lax.fori_loop(1, count, target_finish, 0)
    for k in range(z_size):
        relay(k)
    local[3].wait()
    wait_core(y, x)
    score(y, x)
    relay_diagonal()
    wait_core(1 - y, x)
    score(1 - y, x)
    wait_core(y, 1 - x)
    score(y, 1 - x)
    wait_core(1 - y, 1 - x)
    score(1 - y, 1 - x)

    stat_start, stat_finish = everyone(
        lambda block: stats_out.at[block // per_lane], stats_in.at[me], stat_send, stat_recv
    )
    lax.fori_loop(1, count, stat_start, 0)
    stats_in[me] = stats_out[me // per_lane]
    for copy in pending:
        copy.wait_send()
    for copy in parts:
        copy.wait_send()
    lax.fori_loop(1, count, stat_finish, 0)

    gathered = stats_in[...]
    shares_lse = gathered[:, 0, :]
    top = jnp.max(shares_lse, axis=0, keepdims=True)
    nll = (
        top
        + jnp.log(jnp.sum(jnp.exp(shares_lse - top), axis=0, keepdims=True))
        - jnp.sum(gathered[:, 1, :], axis=0, keepdims=True)
    )
    doc_lanes = ppl_out.shape[1]
    doc_lane = lax.broadcasted_iota(jnp.int32, (1, doc_lanes), 1)
    mine = jnp.zeros((1, doc_lanes), jnp.float32)
    values = []
    for i in range(docs):
        inside = (my_slot >= base[i]) & (my_slot < base[i] + live[i])
        used = jnp.sum(jnp.where(inside, nll, 0.0), axis=1, keepdims=True)
        value = used / jnp.full((1, 1), live[i], jnp.int32).astype(jnp.float32)
        values.append(value)
        mine = jnp.where(doc_lane == me * docs + i, value, mine)
    ppl_out[...] = mine
    ppl_in[me] = mine
    ppl_start, ppl_finish = everyone(lambda block: ppl_out, ppl_in.at[me], ppl_send, ppl_recv)
    lax.fori_loop(1, count, ppl_start, 0)
    lax.fori_loop(1, count, ppl_finish, 0)

    table_ppl = ppl_in[...].reshape(count, doc_lanes)
    row = jnp.sum(table_ppl, axis=0, keepdims=True)
    source = lax.broadcasted_iota(jnp.int32, (count, doc_lanes), 0)
    lanes = lax.broadcasted_iota(jnp.int32, (count, doc_lanes), 1)
    smaller = jnp.zeros((1, doc_lanes), jnp.float32)
    for i in range(docs):
        column = jnp.sum(
            jnp.where(lanes == source * docs + i, table_ppl, 0.0), axis=1, keepdims=True
        )
        smaller = smaller + jnp.sum(jnp.where(column < row, 1.0, 0.0), axis=0, keepdims=True)
    cutoff = jnp.full((1, doc_lanes), cutoff_ref[0], jnp.int32).astype(jnp.float32)
    allowed = (smaller < cutoff) & (doc_lane < count * docs)
    threshold = jnp.max(jnp.where(allowed, row, -3e38), axis=1, keepdims=True)
    shown = lax.broadcasted_iota(jnp.int32, (1, LANES), 1)
    ppl_row = jnp.zeros((1, LANES), jnp.float32)
    for i in range(docs):
        ppl_row = jnp.where(shown == i, values[i], ppl_row)
    ppl_ref[...] = ppl_row
    margin_ref[...] = ppl_row - threshold


def on_device(
    dp_size, vocab_size,
    hidden_in, tokens, lengths, cutoff, norm_gain,
    gate_weight, up_weight, down_weight, final_gain, head_table,
):
    docs, length, width = hidden_in.shape
    count = dp_size * vocab_size
    doc_lanes = -(-count * docs // LANES) * LANES
    bf16, f32 = jnp.bfloat16, jnp.float32
    vmem = pl.BlockSpec(memory_space=pltpu.VMEM)
    smem = pl.BlockSpec(memory_space=pltpu.SMEM)
    hbm = pl.BlockSpec(memory_space=pl.ANY)
    dma = pltpu.SemaphoreType.DMA
    z_size = dp_size // 2
    row_sends = 8 * z_size + 2 * z_size
    log_ppl, margin = pl.pallas_call(
        functools.partial(kernel, dp_size, vocab_size, docs, length),
        out_shape=(jax.ShapeDtypeStruct((1, LANES), f32),) * 2,
        in_specs=[vmem, smem, smem, smem, vmem, vmem, hbm, hbm, hbm, hbm],
        out_specs=(vmem, vmem),
        scratch_shapes=[
            pltpu.VMEM(gate_weight.shape, bf16),
            pltpu.VMEM(up_weight.shape, bf16),
            pltpu.VMEM(down_weight.shape, bf16),
            pltpu.VMEM(head_table.shape, bf16),
            pltpu.VMEM((vocab_size, CAP, width), bf16),
            pltpu.VMEM((vocab_size * CAP, width), f32),
            pltpu.VMEM((vocab_size, CAP, width), bf16),
            pltpu.VMEM((vocab_size, CAP, width), bf16),
            pltpu.VMEM((count, CAP, width), bf16),
            pltpu.VMEM((1, LANES), jnp.int32),
            pltpu.VMEM((count, 1, LANES), jnp.int32),
            pltpu.VMEM((count * CAP // LANES, 2, LANES), f32),
            pltpu.VMEM((count, 2, LANES), f32),
            pltpu.VMEM((1, doc_lanes), f32),
            pltpu.VMEM((count, 1, doc_lanes), f32),
            dma((4,)),
            dma((vocab_size,)), dma((vocab_size,)),
            dma((vocab_size,)), dma((vocab_size,)),
            dma((row_sends,)), dma((count,)),
            dma((count,)), dma((count,)),
            dma((count,)), dma((count,)),
            dma((count,)), dma((count,)),
        ],
        compiler_params=pltpu.CompilerParams(collective_id=0, has_side_effects=True),
        name="whole_step",
    )(
        hidden_in.reshape(docs * length, width), tokens, lengths, cutoff,
        norm_gain.reshape(1, width), final_gain.reshape(1, width),
        gate_weight, up_weight, down_weight, head_table,
    )
    return log_ppl[0, :docs], margin[0, :docs]


def solution(mesh):
    return jax.shard_map(
        functools.partial(on_device, mesh.shape["dp"], mesh.shape["vocab"]),
        mesh=mesh,
        in_specs=(
            P(("dp", "vocab"), None, None),
            P(("dp", "vocab"), None),
            P(("dp", "vocab")),
            P(),
            P(),
            P(None, "vocab"),
            P(None, "vocab"),
            P("vocab", None),
            P(),
            P(("dp", "vocab"), None),
        ),
        out_specs=(P(("dp", "vocab")), P(("dp", "vocab"))),
        check_vma=False,
    )
```

```python
import functools

import jax
import jax.numpy as jnp
from jax import lax
from jax.experimental import pallas as pl
from jax.experimental.pallas import tpu as pltpu
from jax.sharding import PartitionSpec as P

MESH = pl.DeviceIdType.MESH
CAP = 32
LANES = 128


def rms_norm(values, gain):
    squares = jnp.mean(values * values, axis=-1, keepdims=True)
    return values * lax.rsqrt(squares + 1e-06) * gain


def kernel(
    dp_size, vocab_size, docs, length,
    hidden_ref, tokens_ref, lengths_ref, cutoff_ref, norm_gain_ref, final_gain_ref,
    gate_hbm, up_hbm, down_hbm, table_hbm,
    ppl_ref, margin_ref,
    gate, up, down, table, group_rows, acc, part_out, part_in, rows,
    stats_out, stats_in, ppl_out, ppl_in,
    local_sem, group_send, group_recv, part_send, part_recv, row_send, row_recv,
    stat_send, stat_recv, ppl_send, ppl_recv,
):
    dp = lax.axis_index("dp")
    vocab = lax.axis_index("vocab")
    count = dp_size * vocab_size
    z_size = dp_size // 2
    z, y = dp // 2, dp % 2
    x, c = vocab // 2, vocab % 2
    width = hidden_ref.shape[1]
    vocab_rows = table.shape[0]
    per_lane = LANES // CAP

    def block_of(y, x, c, z):
        return ((y * 2 + x) * 2 + c) * z_size + z

    def device_of(block):
        rest = block // z_size
        return (
            (block % z_size) * 2 + rest // 4,
            ((rest // 2) % 2) * 2 + rest % 2,
        )

    me = block_of(y, x, c, z)
    lane_start = (me % per_lane) * CAP

    local = [
        pltpu.make_async_copy(source, target, local_sem.at[i])
        for i, (source, target) in enumerate(
            ((gate_hbm, gate), (up_hbm, up), (down_hbm, down), (table_hbm, table))
        )
    ]
    for copy in local:
        copy.start()

    barrier = pltpu.get_barrier_semaphore()

    partners = [(dp, (vocab + k) % vocab_size) for k in range(1, vocab_size)]
    partners += [((z ^ k) * 2 + y, vocab) for k in range(1, z_size)]
    partners.append((z * 2 + 1 - y, vocab))
    for device in partners:
        pl.semaphore_signal(barrier, inc=1, device_id=device, device_id_type=MESH)

    live = [lengths_ref[i] - 1 for i in range(docs)]
    base = [0]
    for i in range(docs - 1):
        base.append(base[-1] + live[i])
    slot = lax.broadcasted_iota(jnp.int32, (CAP, docs * length), 0)
    position = lax.broadcasted_iota(jnp.int32, (CAP, docs * length), 1)
    chosen = jnp.zeros((CAP, docs * length), jnp.float32)
    lane = lax.broadcasted_iota(jnp.int32, (1, LANES), 1)
    my_slot = lane - lane_start
    target = jnp.zeros((1, LANES), jnp.int32)
    for i in range(docs):
        step = position - i * length
        hit = (step >= 0) & (step < live[i]) & (slot == step + base[i])
        chosen = jnp.where(hit, 1.0, chosen)
        for t in range(length - 1):
            here = (my_slot == base[i] + t) & (t < live[i])
            target = jnp.where(here, tokens_ref[i, t + 1], target)
    packed = jnp.dot(
        chosen.astype(jnp.bfloat16), hidden_ref[...], preferred_element_type=jnp.float32
    )
    group_rows[vocab] = packed.astype(jnp.bfloat16)

    pl.semaphore_wait(barrier, len(partners))

    def group_copy(buffer_from, buffer_to, send, recv, k):
        other = (vocab + k) % vocab_size
        return pltpu.make_async_remote_copy(
            src_ref=buffer_from(other),
            dst_ref=buffer_to,
            send_sem=send.at[k],
            recv_sem=recv.at[k],
            device_id=(dp, other),
            device_id_type=MESH,
        )

    shares = [
        group_copy(lambda other: group_rows.at[vocab], group_rows.at[vocab], group_send, group_recv, k)
        for k in range(1, vocab_size)
    ]
    for copy in shares:
        copy.start()

    def everyone(source, landing, send, recv):
        def make(k):
            block = (me + k) % count
            return pltpu.make_async_remote_copy(
                src_ref=source(block),
                dst_ref=landing,
                send_sem=send.at[k],
                recv_sem=recv.at[k],
                device_id=device_of(block),
                device_id_type=MESH,
            )

        def start(k, carry):
            make(k).start()
            return carry

        def finish(k, carry):
            make(k).wait()
            return carry

        return start, finish

    for copy in shares:
        copy.wait()
    for copy in local[:3]:
        copy.wait()

    all_rows = vocab_size * CAP
    normed = rms_norm(
        group_rows[...].reshape(all_rows, width).astype(jnp.float32), norm_gain_ref[...]
    ).astype(jnp.bfloat16)
    hidden_units = gate.shape[1]
    tile = min(256, hidden_units)
    for j in range(hidden_units // tile):
        units = pl.ds(j * tile, tile)
        gate_part = jnp.dot(normed, gate[:, units], preferred_element_type=jnp.float32)
        up_part = jnp.dot(normed, up[:, units], preferred_element_type=jnp.float32)
        active = (gate_part / (1.0 + jnp.exp(-gate_part)) * up_part).astype(jnp.bfloat16)
        share = jnp.dot(active, down[units, :], preferred_element_type=jnp.float32)
        if j == 0:
            acc[...] = share
        else:
            acc[...] += share
    part_out[...] = acc[...].reshape(vocab_size, CAP, width).astype(jnp.bfloat16)
    parts = [
        group_copy(lambda other: part_out.at[other], part_in.at[vocab], part_send, part_recv, k)
        for k in range(1, vocab_size)
    ]
    for copy in parts:
        copy.start()
    branch = acc[pl.ds(pl.multiple_of(vocab * CAP, CAP), CAP), :]
    for k, copy in enumerate(parts):
        copy.wait_recv()
        branch = branch + part_in[(vocab + vocab_size - 1 - k) % vocab_size].astype(jnp.float32)
    stream = (packed + branch).astype(jnp.bfloat16).astype(jnp.float32)
    final = rms_norm(stream, final_gain_ref[...])
    code = jnp.concatenate(
        [(lax.shift_right_logical(target, 8 * i) & 255).astype(jnp.float32) for i in range(3)]
        + [jnp.zeros((1, width - 3 * LANES), jnp.float32)],
        axis=1,
    )
    last = lax.broadcasted_iota(jnp.int32, (CAP, width), 0) == CAP - 1
    rows[me] = jnp.where(last, code, final).astype(jnp.bfloat16)

    pending = []

    def send_row(block, device):
        copy = pltpu.make_async_remote_copy(
            src_ref=rows.at[block],
            dst_ref=rows.at[block],
            send_sem=row_send.at[len(pending)],
            recv_sem=row_recv.at[block],
            device_id=device,
            device_id_type=MESH,
        )
        copy.start()
        pending.append(copy)

    def wait_row(block):
        pltpu.make_async_remote_copy(
            src_ref=rows.at[block],
            dst_ref=rows.at[block],
            send_sem=row_send.at[0],
            recv_sem=row_recv.at[block],
            device_id=(dp, vocab),
            device_id_type=MESH,
        ).wait_recv()

    other_core = (dp, x * 2 + 1 - c)
    y_peer = (z * 2 + 1 - y, vocab)
    x_peer = (dp, (1 - x) * 2 + c)

    for k in range(1, z_size):
        send_row(me, ((z ^ k) * 2 + y, vocab))
        if k == 1:
            send_row(me, y_peer)
            send_row(me, x_peer)
            send_row(me, other_core)

    def relay_z(k):
        block = block_of(y, x, c, z ^ k)
        wait_row(block)
        send_row(block, y_peer)
        send_row(block, x_peer)
        send_row(block, other_core)

    def relay_sides(k):
        block_y = block_of(1 - y, x, c, z ^ k)
        wait_row(block_y)
        if k % 2:
            send_row(block_y, x_peer)
        send_row(block_y, other_core)
        block_x = block_of(y, 1 - x, c, z ^ k)
        wait_row(block_x)
        if k % 2 == 0:
            send_row(block_x, y_peer)
        send_row(block_x, other_core)

    def relay_diagonal():
        for k in range(z_size):
            block = block_of(1 - y, 1 - x, c, z ^ k)
            wait_row(block)
            send_row(block, other_core)

    def wait_core(y, x):
        for k in range(z_size):
            wait_row(block_of(y, x, 1 - c, k))

    offset = (dp * vocab_size + vocab) * vocab_rows
    chunk = min(1024, vocab_rows)
    set_blocks = min(8, 2 * z_size)
    set_rows = set_blocks * CAP
    lane_sets = set_rows // LANES

    def read_targets(first):
        code = jnp.sum(
            rows[pl.ds(first, per_lane), CAP - 16 :, : 3 * LANES].astype(jnp.float32), axis=0
        )[15:, :]
        low, mid, high = (code[:, i * LANES : (i + 1) * LANES] for i in range(3))
        return (low + 256.0 * mid + 65536.0 * high).astype(jnp.int32)

    def score(y, x):
        def one_set(s, carry):
            first = block_of(y, x, 0, 0) + s * set_blocks
            wanted = jnp.concatenate(
                [
                    read_targets(first + g * per_lane)
                    for g in range(lane_sets)
                ],
                axis=1,
            ) - offset
            sublane = lax.broadcasted_iota(jnp.int32, (8, set_rows), 0)
            wanted = jnp.broadcast_to(wanted, (8, set_rows)) - sublane
            index = lax.broadcasted_iota(jnp.int32, (chunk // 8, 8, set_rows), 0) * 8

            def one_chunk(j, running):
                highest, exp_sum, picked = running
                start = pl.multiple_of(j * chunk, chunk)
                part = rows[pl.ds(first, set_blocks)].reshape(set_rows, width)
                logits = lax.dot_general(
                    table[pl.ds(start, chunk), :],
                    part,
                    (((1,), (1,)), ((), ())),
                    preferred_element_type=jnp.float32,
                ).reshape(chunk // 8, 8, set_rows)
                fresh = jnp.maximum(highest, jnp.max(logits, axis=0))
                exp_sum = exp_sum * jnp.exp(highest - fresh) + jnp.sum(
                    jnp.exp(logits - fresh[None]), axis=0
                )
                picked = picked + jnp.sum(
                    jnp.where(index == (wanted - start)[None], logits, 0.0), axis=0
                )
                return fresh, exp_sum, picked

            blank = jnp.zeros((8, set_rows), jnp.float32)
            highest, exp_sum, picked = lax.fori_loop(
                0, vocab_rows // chunk, one_chunk, (blank - 3e38, blank, blank)
            )
            top = jnp.max(highest, axis=0, keepdims=True)
            total = jnp.sum(exp_sum * jnp.exp(highest - top), axis=0, keepdims=True)
            both = jnp.concatenate(
                [top + jnp.log(total), jnp.sum(picked, axis=0, keepdims=True)], axis=0
            )
            for g in range(lane_sets):
                stats_out[first // per_lane + g] = both[:, g * LANES : (g + 1) * LANES]
            return carry

        lax.fori_loop(0, 2 * z_size // set_blocks, one_set, 0)

    stat_start, stat_finish = everyone(
        lambda block: stats_out.at[block // per_lane], stats_in.at[me], stat_send, stat_recv
    )
    chip_blocks = 2 * z_size
    my_place = me % chip_blocks

    def share_stats(y, x, own):
        def one(j, carry):
            block = block_of(y, x, 0, 0) + (my_place + j) % chip_blocks
            stat_start((block + count - me) % count, 0)
            return carry

        lax.fori_loop(1 if own else 0, chip_blocks, one, 0)

    relay_z(1)
    relay_sides(0)
    relay_sides(1)
    for k in range(2, z_size):
        relay_z(k)
    local[3].wait()
    wait_core(y, x)
    score(y, x)
    share_stats(y, x, True)
    for k in range(2, z_size):
        relay_sides(k)
    wait_core(1 - y, x)
    score(1 - y, x)
    share_stats(1 - y, x, False)
    relay_diagonal()
    wait_core(y, 1 - x)
    score(y, 1 - x)
    share_stats(y, 1 - x, False)
    wait_core(1 - y, 1 - x)
    score(1 - y, 1 - x)
    share_stats(1 - y, 1 - x, False)

    stats_in[me] = stats_out[me // per_lane]
    for copy in pending:
        copy.wait_send()
    for copy in parts:
        copy.wait_send()
    lax.fori_loop(1, count, stat_finish, 0)

    gathered = stats_in[...]
    shares_lse = gathered[:, 0, :]
    top = jnp.max(shares_lse, axis=0, keepdims=True)
    nll = (
        top
        + jnp.log(jnp.sum(jnp.exp(shares_lse - top), axis=0, keepdims=True))
        - jnp.sum(gathered[:, 1, :], axis=0, keepdims=True)
    )
    doc_lanes = ppl_out.shape[1]
    doc_lane = lax.broadcasted_iota(jnp.int32, (1, doc_lanes), 1)
    mine = jnp.zeros((1, doc_lanes), jnp.float32)
    values = []
    for i in range(docs):
        inside = (my_slot >= base[i]) & (my_slot < base[i] + live[i])
        used = jnp.sum(jnp.where(inside, nll, 0.0), axis=1, keepdims=True)
        value = used / jnp.full((1, 1), live[i], jnp.int32).astype(jnp.float32)
        values.append(value)
        mine = jnp.where(doc_lane == me * docs + i, value, mine)
    ppl_out[...] = mine
    ppl_in[me] = mine
    ppl_start, ppl_finish = everyone(lambda block: ppl_out, ppl_in.at[me], ppl_send, ppl_recv)
    lax.fori_loop(1, count, ppl_start, 0)
    lax.fori_loop(1, count, ppl_finish, 0)

    table_ppl = ppl_in[...].reshape(count, doc_lanes)
    row = jnp.sum(table_ppl, axis=0, keepdims=True)
    source = lax.broadcasted_iota(jnp.int32, (count, doc_lanes), 0)
    lanes = lax.broadcasted_iota(jnp.int32, (count, doc_lanes), 1)
    smaller = jnp.zeros((1, doc_lanes), jnp.float32)
    for i in range(docs):
        column = jnp.sum(
            jnp.where(lanes == source * docs + i, table_ppl, 0.0), axis=1, keepdims=True
        )
        smaller = smaller + jnp.sum(jnp.where(column < row, 1.0, 0.0), axis=0, keepdims=True)
    cutoff = jnp.full((1, doc_lanes), cutoff_ref[0], jnp.int32).astype(jnp.float32)
    allowed = (smaller < cutoff) & (doc_lane < count * docs)
    threshold = jnp.max(jnp.where(allowed, row, -3e38), axis=1, keepdims=True)
    shown = lax.broadcasted_iota(jnp.int32, (1, LANES), 1)
    ppl_row = jnp.zeros((1, LANES), jnp.float32)
    for i in range(docs):
        ppl_row = jnp.where(shown == i, values[i], ppl_row)
    ppl_ref[...] = ppl_row
    margin_ref[...] = ppl_row - threshold


def on_device(
    dp_size, vocab_size,
    hidden_in, tokens, lengths, cutoff, norm_gain,
    gate_weight, up_weight, down_weight, final_gain, head_table,
):
    docs, length, width = hidden_in.shape
    count = dp_size * vocab_size
    doc_lanes = -(-count * docs // LANES) * LANES
    bf16, f32 = jnp.bfloat16, jnp.float32
    vmem = pl.BlockSpec(memory_space=pltpu.VMEM)
    smem = pl.BlockSpec(memory_space=pltpu.SMEM)
    hbm = pl.BlockSpec(memory_space=pl.ANY)
    dma = pltpu.SemaphoreType.DMA
    z_size = dp_size // 2
    row_sends = 8 * z_size + 2 * z_size
    log_ppl, margin = pl.pallas_call(
        functools.partial(kernel, dp_size, vocab_size, docs, length),
        out_shape=(jax.ShapeDtypeStruct((1, LANES), f32),) * 2,
        in_specs=[vmem, smem, smem, smem, vmem, vmem, hbm, hbm, hbm, hbm],
        out_specs=(vmem, vmem),
        scratch_shapes=[
            pltpu.VMEM(gate_weight.shape, bf16),
            pltpu.VMEM(up_weight.shape, bf16),
            pltpu.VMEM(down_weight.shape, bf16),
            pltpu.VMEM(head_table.shape, bf16),
            pltpu.VMEM((vocab_size, CAP, width), bf16),
            pltpu.VMEM((vocab_size * CAP, width), f32),
            pltpu.VMEM((vocab_size, CAP, width), bf16),
            pltpu.VMEM((vocab_size, CAP, width), bf16),
            pltpu.VMEM((count, CAP, width), bf16),
            pltpu.VMEM((count * CAP // LANES, 2, LANES), f32),
            pltpu.VMEM((count, 2, LANES), f32),
            pltpu.VMEM((1, doc_lanes), f32),
            pltpu.VMEM((count, 1, doc_lanes), f32),
            dma((4,)),
            dma((vocab_size,)), dma((vocab_size,)),
            dma((vocab_size,)), dma((vocab_size,)),
            dma((row_sends,)), dma((count,)),
            dma((count,)), dma((count,)),
            dma((count,)), dma((count,)),
        ],
        compiler_params=pltpu.CompilerParams(collective_id=0, has_side_effects=True),
        name="whole_step",
    )(
        hidden_in.reshape(docs * length, width), tokens, lengths, cutoff,
        norm_gain.reshape(1, width), final_gain.reshape(1, width),
        gate_weight, up_weight, down_weight, head_table,
    )
    return log_ppl[0, :docs], margin[0, :docs]


def solution(mesh):
    return jax.shard_map(
        functools.partial(on_device, mesh.shape["dp"], mesh.shape["vocab"]),
        mesh=mesh,
        in_specs=(
            P(("dp", "vocab"), None, None),
            P(("dp", "vocab"), None),
            P(("dp", "vocab")),
            P(),
            P(),
            P(None, "vocab"),
            P(None, "vocab"),
            P("vocab", None),
            P(),
            P(("dp", "vocab"), None),
        ),
        out_specs=(P(("dp", "vocab")), P(("dp", "vocab"))),
        check_vma=False,
    )
```

```python
import functools

import jax
import jax.numpy as jnp
from jax import lax
from jax.experimental import pallas as pl
from jax.experimental.pallas import tpu as pltpu
from jax.sharding import PartitionSpec as P

MESH = pl.DeviceIdType.MESH
CAP = 32
LANES = 128


def rms_norm(values, gain):
    squares = jnp.mean(values * values, axis=-1, keepdims=True)
    return values * lax.rsqrt(squares + 1e-06) * gain


def kernel(
    dp_size, vocab_size, docs, length,
    hidden_ref, tokens_ref, lengths_ref, cutoff_ref, norm_gain_ref, final_gain_ref,
    gate_hbm, up_hbm, down_hbm, table_hbm,
    ppl_ref, margin_ref,
    gate, up, down, table, group_rows, acc, part_out, part_in, rows,
    stats_out, stats_in, ppl_out, ppl_in,
    local_sem, group_send, group_recv, part_send, part_recv, row_send, row_recv,
    stat_send, stat_recv, ppl_send, ppl_recv,
):
    dp = lax.axis_index("dp")
    vocab = lax.axis_index("vocab")
    count = dp_size * vocab_size
    z_size = dp_size // 2
    z, y = dp // 2, dp % 2
    x, c = vocab // 2, vocab % 2
    width = hidden_ref.shape[1]
    vocab_rows = table.shape[0]
    per_lane = LANES // CAP

    def block_of(y, x, c, z):
        return ((y * 2 + x) * 2 + c) * z_size + z

    def device_of(block):
        rest = block // z_size
        return (
            (block % z_size) * 2 + rest // 4,
            ((rest // 2) % 2) * 2 + rest % 2,
        )

    me = block_of(y, x, c, z)
    lane_start = (me % per_lane) * CAP

    local = [
        pltpu.make_async_copy(source, target, local_sem.at[i])
        for i, (source, target) in enumerate(
            ((gate_hbm, gate), (up_hbm, up), (down_hbm, down), (table_hbm, table))
        )
    ]
    for copy in local:
        copy.start()

    barrier = pltpu.get_barrier_semaphore()

    partners = [(dp, (vocab + k) % vocab_size) for k in range(1, vocab_size)]
    partners += [((z ^ k) * 2 + y, vocab) for k in range(1, z_size)]
    partners.append((z * 2 + 1 - y, vocab))
    for device in partners:
        pl.semaphore_signal(barrier, inc=1, device_id=device, device_id_type=MESH)

    live = [lengths_ref[i] - 1 for i in range(docs)]
    base = [0]
    for i in range(docs - 1):
        base.append(base[-1] + live[i])
    slot = lax.broadcasted_iota(jnp.int32, (CAP, docs * length), 0)
    position = lax.broadcasted_iota(jnp.int32, (CAP, docs * length), 1)
    chosen = jnp.zeros((CAP, docs * length), jnp.float32)
    lane = lax.broadcasted_iota(jnp.int32, (1, LANES), 1)
    my_slot = lane - lane_start
    target = jnp.zeros((1, LANES), jnp.int32)
    for i in range(docs):
        step = position - i * length
        hit = (step >= 0) & (step < live[i]) & (slot == step + base[i])
        chosen = jnp.where(hit, 1.0, chosen)
        for t in range(length - 1):
            here = (my_slot == base[i] + t) & (t < live[i])
            target = jnp.where(here, tokens_ref[i, t + 1], target)
    packed = jnp.dot(
        chosen.astype(jnp.bfloat16), hidden_ref[...], preferred_element_type=jnp.float32
    )
    group_rows[vocab] = packed.astype(jnp.bfloat16)

    pl.semaphore_wait(barrier, len(partners))

    def group_copy(buffer_from, buffer_to, send, recv, k):
        other = (vocab + k) % vocab_size
        return pltpu.make_async_remote_copy(
            src_ref=buffer_from(other),
            dst_ref=buffer_to,
            send_sem=send.at[k],
            recv_sem=recv.at[k],
            device_id=(dp, other),
            device_id_type=MESH,
        )

    shares = [
        group_copy(lambda other: group_rows.at[vocab], group_rows.at[vocab], group_send, group_recv, k)
        for k in range(1, vocab_size)
    ]
    for copy in shares:
        copy.start()

    def everyone(source, landing, send, recv):
        def make(k):
            block = (me + k) % count
            return pltpu.make_async_remote_copy(
                src_ref=source(block),
                dst_ref=landing,
                send_sem=send.at[k],
                recv_sem=recv.at[k],
                device_id=device_of(block),
                device_id_type=MESH,
            )

        def start(k, carry):
            make(k).start()
            return carry

        def finish(k, carry):
            make(k).wait()
            return carry

        return start, finish

    for copy in shares:
        copy.wait_recv()
    for copy in local[:3]:
        copy.wait()

    all_rows = vocab_size * CAP
    normed = rms_norm(
        group_rows[...].reshape(all_rows, width).astype(jnp.float32), norm_gain_ref[...]
    ).astype(jnp.bfloat16)
    hidden_units = gate.shape[1]
    tile = min(256, hidden_units)
    for j in range(hidden_units // tile):
        units = pl.ds(j * tile, tile)
        gate_part = jnp.dot(normed, gate[:, units], preferred_element_type=jnp.float32)
        up_part = jnp.dot(normed, up[:, units], preferred_element_type=jnp.float32)
        active = (gate_part / (1.0 + jnp.exp(-gate_part)) * up_part).astype(jnp.bfloat16)
        share = jnp.dot(active, down[units, :], preferred_element_type=jnp.float32)
        if j == 0:
            acc[...] = share
        else:
            acc[...] += share
    part_out[...] = acc[...].reshape(vocab_size, CAP, width).astype(jnp.bfloat16)
    parts = [
        group_copy(lambda other: part_out.at[other], part_in.at[vocab], part_send, part_recv, k)
        for k in range(1, vocab_size)
    ]
    for copy in parts:
        copy.start()
    branch = acc[pl.ds(pl.multiple_of(vocab * CAP, CAP), CAP), :]
    for k, copy in enumerate(parts):
        copy.wait_recv()
        branch = branch + part_in[(vocab + vocab_size - 1 - k) % vocab_size].astype(jnp.float32)
    stream = (packed + branch).astype(jnp.bfloat16).astype(jnp.float32)
    final = rms_norm(stream, final_gain_ref[...])
    code = jnp.concatenate(
        [(lax.shift_right_logical(target, 8 * i) & 255).astype(jnp.float32) for i in range(3)]
        + [jnp.zeros((1, width - 3 * LANES), jnp.float32)],
        axis=1,
    )
    last = lax.broadcasted_iota(jnp.int32, (CAP, width), 0) == CAP - 1
    rows[me] = jnp.where(last, code, final).astype(jnp.bfloat16)

    pending = []

    def send_row(block, device):
        copy = pltpu.make_async_remote_copy(
            src_ref=rows.at[block],
            dst_ref=rows.at[block],
            send_sem=row_send.at[len(pending)],
            recv_sem=row_recv.at[block],
            device_id=device,
            device_id_type=MESH,
        )
        copy.start()
        pending.append(copy)

    def wait_row(block):
        pltpu.make_async_remote_copy(
            src_ref=rows.at[block],
            dst_ref=rows.at[block],
            send_sem=row_send.at[0],
            recv_sem=row_recv.at[block],
            device_id=(dp, vocab),
            device_id_type=MESH,
        ).wait_recv()

    other_core = (dp, x * 2 + 1 - c)
    y_peer = (z * 2 + 1 - y, vocab)
    x_peer = (dp, (1 - x) * 2 + c)

    for k in range(1, z_size):
        send_row(me, ((z ^ k) * 2 + y, vocab))
        if k == 1:
            send_row(me, y_peer)
            send_row(me, x_peer)
            send_row(me, other_core)

    def relay_z(k):
        block = block_of(y, x, c, z ^ k)
        wait_row(block)
        send_row(block, y_peer)
        send_row(block, x_peer)
        send_row(block, other_core)

    def relay_sides(k):
        block_y = block_of(1 - y, x, c, z ^ k)
        wait_row(block_y)
        if k % 2:
            send_row(block_y, x_peer)
        send_row(block_y, other_core)
        block_x = block_of(y, 1 - x, c, z ^ k)
        wait_row(block_x)
        if k % 2 == 0:
            send_row(block_x, y_peer)
        send_row(block_x, other_core)

    def relay_diagonal():
        for k in range(z_size):
            block = block_of(1 - y, 1 - x, c, z ^ k)
            wait_row(block)
            send_row(block, other_core)

    def wait_core(y, x):
        for k in range(z_size):
            wait_row(block_of(y, x, 1 - c, k))

    offset = (dp * vocab_size + vocab) * vocab_rows
    chunk = min(1024, vocab_rows)
    set_blocks = min(8, 2 * z_size)
    set_rows = set_blocks * CAP
    lane_sets = set_rows // LANES

    def read_targets(first):
        code = jnp.sum(
            rows[pl.ds(first, per_lane), CAP - 16 :, : 3 * LANES].astype(jnp.float32), axis=0
        )[15:, :]
        low, mid, high = (code[:, i * LANES : (i + 1) * LANES] for i in range(3))
        return (low + 256.0 * mid + 65536.0 * high).astype(jnp.int32)

    def score(y, x):
        def one_set(s, carry):
            first = block_of(y, x, 0, 0) + s * set_blocks
            wanted = jnp.concatenate(
                [
                    read_targets(first + g * per_lane)
                    for g in range(lane_sets)
                ],
                axis=1,
            ) - offset
            sublane = lax.broadcasted_iota(jnp.int32, (8, set_rows), 0)
            wanted = jnp.broadcast_to(wanted, (8, set_rows)) - sublane
            index = lax.broadcasted_iota(jnp.int32, (chunk // 8, 8, set_rows), 0) * 8

            def one_chunk(j, running):
                highest, exp_sum, picked = running
                start = pl.multiple_of(j * chunk, chunk)
                part = rows[pl.ds(first, set_blocks)].reshape(set_rows, width)
                logits = lax.dot_general(
                    table[pl.ds(start, chunk), :],
                    part,
                    (((1,), (1,)), ((), ())),
                    preferred_element_type=jnp.float32,
                ).reshape(chunk // 8, 8, set_rows)
                fresh = jnp.maximum(highest, jnp.max(logits, axis=0))
                exp_sum = exp_sum * jnp.exp(highest - fresh) + jnp.sum(
                    jnp.exp(logits - fresh[None]), axis=0
                )
                picked = picked + jnp.sum(
                    jnp.where(index == (wanted - start)[None], logits, 0.0), axis=0
                )
                return fresh, exp_sum, picked

            blank = jnp.zeros((8, set_rows), jnp.float32)
            highest, exp_sum, picked = lax.fori_loop(
                0, vocab_rows // chunk, one_chunk, (blank - 3e38, blank, blank)
            )
            top = jnp.max(highest, axis=0, keepdims=True)
            total = jnp.sum(exp_sum * jnp.exp(highest - top), axis=0, keepdims=True)
            both = jnp.concatenate(
                [top + jnp.log(total), jnp.sum(picked, axis=0, keepdims=True)], axis=0
            )
            for g in range(lane_sets):
                stats_out[first // per_lane + g] = both[:, g * LANES : (g + 1) * LANES]
            return carry

        lax.fori_loop(0, 2 * z_size // set_blocks, one_set, 0)

    stat_start, stat_finish = everyone(
        lambda block: stats_out.at[block // per_lane], stats_in.at[me], stat_send, stat_recv
    )
    chip_blocks = 2 * z_size
    my_place = me % chip_blocks

    def share_stats(y, x, own):
        def one(j, carry):
            block = block_of(y, x, 0, 0) + (my_place + j) % chip_blocks
            stat_start((block + count - me) % count, 0)
            return carry

        lax.fori_loop(1 if own else 0, chip_blocks, one, 0)

    relay_z(1)
    relay_sides(0)
    for k in range(2, z_size):
        relay_z(k)
        if k - 1 < z_size // 2:
            relay_sides(k - 1)
    local[3].wait()
    wait_core(y, x)
    score(y, x)
    share_stats(y, x, True)
    for k in range(z_size // 2, z_size):
        relay_sides(k)
    wait_core(1 - y, x)
    score(1 - y, x)
    share_stats(1 - y, x, False)
    relay_diagonal()
    wait_core(y, 1 - x)
    score(y, 1 - x)
    share_stats(y, 1 - x, False)
    wait_core(1 - y, 1 - x)
    score(1 - y, 1 - x)
    share_stats(1 - y, 1 - x, False)

    stats_in[me] = stats_out[me // per_lane]
    for copy in pending:
        copy.wait_send()
    for copy in shares + parts:
        copy.wait_send()
    lax.fori_loop(1, count, stat_finish, 0)

    gathered = stats_in[...]
    shares_lse = gathered[:, 0, :]
    top = jnp.max(shares_lse, axis=0, keepdims=True)
    nll = (
        top
        + jnp.log(jnp.sum(jnp.exp(shares_lse - top), axis=0, keepdims=True))
        - jnp.sum(gathered[:, 1, :], axis=0, keepdims=True)
    )
    doc_lanes = ppl_out.shape[1]
    doc_lane = lax.broadcasted_iota(jnp.int32, (1, doc_lanes), 1)
    mine = jnp.zeros((1, doc_lanes), jnp.float32)
    values = []
    for i in range(docs):
        inside = (my_slot >= base[i]) & (my_slot < base[i] + live[i])
        used = jnp.sum(jnp.where(inside, nll, 0.0), axis=1, keepdims=True)
        value = used / jnp.full((1, 1), live[i], jnp.int32).astype(jnp.float32)
        values.append(value)
        mine = jnp.where(doc_lane == me * docs + i, value, mine)
    ppl_out[...] = mine
    ppl_in[me] = mine
    ppl_start, ppl_finish = everyone(lambda block: ppl_out, ppl_in.at[me], ppl_send, ppl_recv)
    lax.fori_loop(1, count, ppl_start, 0)
    lax.fori_loop(1, count, ppl_finish, 0)

    table_ppl = ppl_in[...].reshape(count, doc_lanes)
    row = jnp.sum(table_ppl, axis=0, keepdims=True)
    source = lax.broadcasted_iota(jnp.int32, (count, doc_lanes), 0)
    lanes = lax.broadcasted_iota(jnp.int32, (count, doc_lanes), 1)
    smaller = jnp.zeros((1, doc_lanes), jnp.float32)
    for i in range(docs):
        column = jnp.sum(
            jnp.where(lanes == source * docs + i, table_ppl, 0.0), axis=1, keepdims=True
        )
        smaller = smaller + jnp.sum(jnp.where(column < row, 1.0, 0.0), axis=0, keepdims=True)
    cutoff = jnp.full((1, doc_lanes), cutoff_ref[0], jnp.int32).astype(jnp.float32)
    allowed = (smaller < cutoff) & (doc_lane < count * docs)
    threshold = jnp.max(jnp.where(allowed, row, -3e38), axis=1, keepdims=True)
    shown = lax.broadcasted_iota(jnp.int32, (1, LANES), 1)
    ppl_row = jnp.zeros((1, LANES), jnp.float32)
    for i in range(docs):
        ppl_row = jnp.where(shown == i, values[i], ppl_row)
    ppl_ref[...] = ppl_row
    margin_ref[...] = ppl_row - threshold


def on_device(
    dp_size, vocab_size,
    hidden_in, tokens, lengths, cutoff, norm_gain,
    gate_weight, up_weight, down_weight, final_gain, head_table,
):
    docs, length, width = hidden_in.shape
    count = dp_size * vocab_size
    doc_lanes = -(-count * docs // LANES) * LANES
    bf16, f32 = jnp.bfloat16, jnp.float32
    vmem = pl.BlockSpec(memory_space=pltpu.VMEM)
    smem = pl.BlockSpec(memory_space=pltpu.SMEM)
    hbm = pl.BlockSpec(memory_space=pl.ANY)
    dma = pltpu.SemaphoreType.DMA
    z_size = dp_size // 2
    row_sends = 8 * z_size + 2 * z_size
    log_ppl, margin = pl.pallas_call(
        functools.partial(kernel, dp_size, vocab_size, docs, length),
        out_shape=(jax.ShapeDtypeStruct((1, LANES), f32),) * 2,
        in_specs=[vmem, smem, smem, smem, vmem, vmem, hbm, hbm, hbm, hbm],
        out_specs=(vmem, vmem),
        scratch_shapes=[
            pltpu.VMEM(gate_weight.shape, bf16),
            pltpu.VMEM(up_weight.shape, bf16),
            pltpu.VMEM(down_weight.shape, bf16),
            pltpu.VMEM(head_table.shape, bf16),
            pltpu.VMEM((vocab_size, CAP, width), bf16),
            pltpu.VMEM((vocab_size * CAP, width), f32),
            pltpu.VMEM((vocab_size, CAP, width), bf16),
            pltpu.VMEM((vocab_size, CAP, width), bf16),
            pltpu.VMEM((count, CAP, width), bf16),
            pltpu.VMEM((count * CAP // LANES, 2, LANES), f32),
            pltpu.VMEM((count, 2, LANES), f32),
            pltpu.VMEM((1, doc_lanes), f32),
            pltpu.VMEM((count, 1, doc_lanes), f32),
            dma((4,)),
            dma((vocab_size,)), dma((vocab_size,)),
            dma((vocab_size,)), dma((vocab_size,)),
            dma((row_sends,)), dma((count,)),
            dma((count,)), dma((count,)),
            dma((count,)), dma((count,)),
        ],
        compiler_params=pltpu.CompilerParams(collective_id=0, has_side_effects=True),
        name="whole_step",
    )(
        hidden_in.reshape(docs * length, width), tokens, lengths, cutoff,
        norm_gain.reshape(1, width), final_gain.reshape(1, width),
        gate_weight, up_weight, down_weight, head_table,
    )
    return log_ppl[0, :docs], margin[0, :docs]


def solution(mesh):
    return jax.shard_map(
        functools.partial(on_device, mesh.shape["dp"], mesh.shape["vocab"]),
        mesh=mesh,
        in_specs=(
            P(("dp", "vocab"), None, None),
            P(("dp", "vocab"), None),
            P(("dp", "vocab")),
            P(),
            P(),
            P(None, "vocab"),
            P(None, "vocab"),
            P("vocab", None),
            P(),
            P(("dp", "vocab"), None),
        ),
        out_specs=(P(("dp", "vocab")), P(("dp", "vocab"))),
        check_vma=False,
    )
```
